32 devices in a mesh: tm: 4 (over y, x), pair: 8 (over z, core).
Axes of the slice: x: 2, y: 2, z: 4, core: 2. Of those that a mesh axis runs over, the one named last changes fastest.
Arguments:
- three_center: bfloat16 [192, 64, 1024], P('pair'), may hold values from -6 to 6
- green_occ: bfloat16 [4, 64, 64, 64], P('tm'), may hold values from -0.75 to 0.75
- green_vir: bfloat16 [4, 64, 64, 64], P('tm'), may hold values from -0.75 to 0.75
- pair_list: int32 [192], P('pair'), may hold values from 0 to 63
- block_counts: int32 [8], P('pair'), may hold values from 6 to 24, as said below
- cosine_weights: float32 [4, 4], replicated, may hold values from -3 to 3
- coulomb_rows: int32 [8, 3], replicated, may hold values from 0 to 7, as said below
- coulomb_blocks: float32 [8, 3, 128, 128], replicated, may hold values from -0.3125 to 0.3125
Outputs:
- screened: float32 [4, 1024, 1024], P('tm', 'pair')
The draws below stay inside these ranges and needn't reach their ends.
Inputs may be any that keep to these rules, and one draw needn't show every extreme that they name: `block_counts`: slots from the count on are not used; some index of pair has all 24 slots live. `coulomb_rows`: the row blocks of one column block are distinct, and the first is the column block itself.
All inputs are finite; a program needn't handle non-finite values.
Results may differ from the reference program's by a relative error of at most 0.0041.
Values sent between devices are 32-bit elements; how exact they have to be, the bound alone decides.
A program may use at most 64 MiB of HBM per device.

```python
import math
import jax
import jax.numpy as jnp
from jax import lax

PANEL = 1024
BW = 64
NGRP = 64
NB_DEV = 24
CB = 128
KPC = 3
NBLK = 192
TIMES = 4
FREQS = 4
NCOLB = 8
N_PAIR = 8


def draw_block_counts(key, part):
    count_key, full_key = jax.random.split(key)
    lowest = max(1, NB_DEV // 4)
    counts = jax.random.randint(count_key, (N_PAIR,), lowest, NB_DEV + 1)
    full_index = jax.random.randint(full_key, (), 0, N_PAIR)
    return counts.at[full_index].set(NB_DEV).astype(jnp.int32)


def draw_coulomb_rows(key, part):

    def single_column(column):
        shuffled = jax.random.permutation(jax.random.fold_in(key, column), NCOLB - 1)
        others = (column + 1 + shuffled[:KPC - 1]) % NCOLB
        return jnp.concatenate([column[None], others.astype(jnp.int32)])
    return jax.vmap(single_column)(jnp.arange(NCOLB, dtype=jnp.int32)).astype(jnp.int32)


def set_ends(array, stream_key, smallest, top_value):
    dims = array.shape
    place = [jax.random.randint(jax.random.fold_in(stream_key, axis), (), 0, dims[axis]) for axis in range(len(dims))]
    array = array.at[tuple(place)].set(smallest)
    longest = dims.index(max(dims))
    place[longest] = (place[longest] + 1) % dims[longest]
    return array.at[tuple(place)].set(top_value)


def with_spikes(result, key, source, target, blocks, factor):
    def block_of(axis_at):
        return (jnp.arange(result.shape[axis_at]) // (result.shape[axis_at] // blocks)).reshape((-1,) + (1,) * (result.ndim - 1 - axis_at))

    first = jax.random.permutation(key, blocks)[block_of(target)]
    other_side = (block_of(target) + blocks // 2) % blocks
    return jnp.where((block_of(source) == first) | (block_of(source) == other_side), factor * result, result)


def shard_levels(rng, shape, cuts, least, top_value):
    def one(axis_at, blocks):
        draws = jax.random.uniform(jax.random.fold_in(jax.random.fold_in(rng, 6), axis_at), (blocks,), jnp.float32, least / len(cuts), top_value / len(cuts))
        return jnp.repeat(jnp.exp(draws), shape[axis_at] // blocks).reshape((-1,) + (1,) * (len(shape) - axis_at - 1))

    factor_of = one(*cuts[0])
    for cut in cuts[1:]:
        factor_of = factor_of * one(*cut)
    return factor_of


def scatter_about(stream_key, shape, width, reach, cuts=(), kind=jnp.bfloat16):
    factor_of = shard_levels(stream_key, shape, cuts, -0.22, 0.18) if cuts else 1.0
    values = jax.random.normal(stream_key, shape, jnp.float32) * width * factor_of
    return jnp.minimum(jnp.maximum(values, -reach), reach).astype(kind)


def heavy_noise(stream_key, extent, width, limit, shards, heavy, kind=jnp.bfloat16):
    result = width * jax.random.normal(stream_key, extent, jnp.float32)
    if shards:
        result = result * shard_levels(stream_key, extent, shards, -0.22, 0.18)
    return jnp.clip(with_spikes(result, jax.random.fold_in(stream_key, 3), *heavy), -limit, limit).astype(kind)


def setup_inputs(seed: int = 0) -> dict:
    arg_keys = jax.random.split(jax.random.key(seed), 9)
    three_center = heavy_noise(arg_keys[0], (NBLK, BW, PANEL), 1.0, 6.0, ((0, 8),), (0, 2, 8, 2.0))
    green_occ = scatter_about(arg_keys[1], (TIMES, NGRP, BW, BW), BW ** -0.5, 0.75, ((0, 4),))
    green_vir = scatter_about(arg_keys[2], (TIMES, NGRP, BW, BW), BW ** -0.5, 0.75, ((0, 4),))
    pair_list = set_ends(jax.random.randint(arg_keys[3], (NBLK,), 0, NGRP), jax.random.fold_in(arg_keys[3], 1), 0, NGRP - 1).astype(jnp.int32)
    block_counts = draw_block_counts(jax.random.fold_in(arg_keys[8], 71), 0)
    cosine_weights = scatter_about(arg_keys[5], (FREQS, TIMES), TIMES ** -0.5, 3.0, (), jnp.float32)
    coulomb_rows = draw_coulomb_rows(jax.random.fold_in(arg_keys[8], 71), 0)
    coulomb_blocks = scatter_about(arg_keys[7], (NCOLB, KPC, CB, CB), (KPC * CB) ** -0.5, 0.3125, (), jnp.float32)
    return dict(three_center=three_center, green_occ=green_occ, green_vir=green_vir, pair_list=pair_list, block_counts=block_counts, cosine_weights=cosine_weights, coulomb_rows=coulomb_rows, coulomb_blocks=coulomb_blocks)


def reference(three_center, green_occ, green_vir, pair_list, block_counts, cosine_weights, coulomb_rows, coulomb_blocks):
    slot_index = jnp.arange(NBLK, dtype=jnp.int32)
    alive_mask = (slot_index % NB_DEV < block_counts[slot_index // NB_DEV]).astype(jnp.float32)
    expanded = three_center.astype(jnp.float32)
    normalizer = 1.0 / math.sqrt(NBLK * BW)

    def half_product(green_matrix):
        picked = green_matrix[pair_list].astype(jnp.float32)
        product = jnp.einsum('bij,bjp->bip', picked, expanded)
        product = product * alive_mask[:, None, None]
        return product.astype(jnp.bfloat16).reshape(NBLK * BW, PANEL)

    def single_time(greens):
        left_side = half_product(greens[0])
        right_side = half_product(greens[1])
        summed = lax.dot_general(left_side, right_side, (((0,), (0,)), ((), ())), preferred_element_type=jnp.float32)
        return summed * normalizer
    panels = lax.map(single_time, (green_occ, green_vir))
    spectra = jnp.einsum('ft,tpq->fpq', cosine_weights, panels, precision=lax.Precision.HIGHEST)
    blocked = spectra.reshape(FREQS * PANEL, NCOLB, CB)
    gathered = jnp.take(blocked, coulomb_rows.reshape(-1), axis=1)
    screened = jnp.einsum('mjx,jxy->mjy', gathered, coulomb_blocks.reshape(NCOLB * KPC, CB, CB), precision=lax.Precision.HIGHEST)
    return screened.reshape(FREQS * PANEL, NCOLB, KPC, CB).sum(axis=2).reshape(FREQS, PANEL, PANEL)
```

```python
import functools
import math

import jax
import jax.numpy as jnp
from jax import lax
from jax.experimental import pallas as pl
from jax.experimental.pallas import tpu as pltpu
from jax.sharding import PartitionSpec as P

MESH = pl.DeviceIdType.MESH


def half_product(green_matrix, pair_list, alive_mask, three_center):
    picked = green_matrix[0][pair_list]
    product = jnp.einsum("bij,bjp->bip", picked, three_center, preferred_element_type=jnp.float32)
    product = product * alive_mask[:, None, None]
    return product.astype(jnp.bfloat16).reshape(-1, three_center.shape[2])


def collective_form(
    three_center,
    green_occ,
    green_vir,
    pair_list,
    block_counts,
    cosine_weights,
    coulomb_rows,
    coulomb_blocks,
):
    slots = three_center.shape[0]
    pair_devices = lax.axis_size("pair")
    alive_mask = (jnp.arange(slots, dtype=jnp.int32) < block_counts[0]).astype(jnp.float32)
    left_side = half_product(green_occ, pair_list, alive_mask, three_center)
    right_side = half_product(green_vir, pair_list, alive_mask, three_center)
    normalizer = 1.0 / math.sqrt(slots * three_center.shape[1] * pair_devices)
    summed = lax.dot_general(
        left_side, right_side, (((0,), (0,)), ((), ())), preferred_element_type=jnp.float32
    )
    row_slab = lax.psum_scatter(summed * normalizer, "pair", scatter_dimension=0, tiled=True)
    transformed = jnp.einsum(
        "ft,trc->frc",
        cosine_weights,
        lax.all_to_all(row_slab[None], "tm", split_axis=2, concat_axis=0, tiled=True),
        precision=lax.Precision.HIGHEST,
    )
    spectra = lax.all_to_all(transformed, "tm", split_axis=0, concat_axis=2, tiled=True)
    rows_here = spectra.shape[1]
    column_blocks = coulomb_rows.shape[0]
    per_column = coulomb_rows.shape[1]
    block_width = coulomb_blocks.shape[2]
    blocked = spectra.reshape(rows_here, column_blocks, block_width)
    gathered = jnp.take(blocked, coulomb_rows.reshape(-1), axis=1)
    factors = coulomb_blocks.reshape(column_blocks * per_column, block_width, block_width)
    screened = jnp.einsum("mjx,jxy->mjy", gathered, factors, precision=lax.Precision.HIGHEST)
    screened = screened.reshape(rows_here, column_blocks, per_column, block_width).sum(axis=2)
    return screened.reshape(1, rows_here, column_blocks * block_width)


def kernel(
    times,
    chips,
    normalizer,
    pair_list_ref,
    counts_ref,
    weights_ref,
    factor_rows_ref,
    three_ref,
    occ_ref,
    vir_ref,
    coulomb_ref,
    out_ref,
    left,
    right,
    to_partner,
    from_partner,
    sums,
    arrived,
    peers_in,
    spectra,
    coulomb_high,
    coulomb_low,
    partner_send,
    partner_recv,
    chain_send,
    chain_recv,
    peer_send,
    peer_recv,
):
    slots, width, panel = three_ref.shape
    pieces, piece_rows = sums.shape[1], sums.shape[2]
    rows = pieces * piece_rows
    me = lax.axis_index("tm")
    place = lax.axis_index("pair")
    z = place // 2
    core = place % 2
    partner = z * 2 + 1 - core

    barrier = pltpu.get_barrier_semaphore()
    pl.semaphore_signal(barrier, inc=1, device_id={"pair": partner}, device_id_type=MESH)
    for offset in range(1, times):
        pl.semaphore_signal(
            barrier, inc=1, device_id={"tm": (me + offset) % times}, device_id_type=MESH
        )

    @pl.when(z > 0)
    def _():
        pl.semaphore_signal(barrier, inc=1, device_id={"pair": place - 2}, device_id_type=MESH)

    @pl.when(z < chips - 1)
    def _():
        pl.semaphore_signal(barrier, inc=1, device_id={"pair": place + 2}, device_id_type=MESH)

    def half(slot, carry):
        group = pair_list_ref[slot]
        alive = (slot < counts_ref[0]).astype(jnp.float32)
        both = jnp.concatenate([occ_ref[0, group], vir_ref[0, group]], axis=0)
        product = jnp.dot(both, three_ref[slot], preferred_element_type=jnp.float32) * alive
        product = product.astype(jnp.bfloat16)
        here = pl.ds(pl.multiple_of(slot * width, width), width)
        left[here, :] = product[:width]
        right[here, :] = product[width:]
        return carry

    lax.fori_loop(0, slots, half, 0)

    neighbours = (z > 0).astype(jnp.int32) + (z < chips - 1).astype(jnp.int32)
    pl.semaphore_wait(barrier, times + neighbours)

    def panel_slab(slab):
        columns = pl.ds(pl.multiple_of(slab * rows, rows), rows)
        product = lax.dot_general(
            left[:, columns],
            right[...],
            (((0,), (0,)), ((), ())),
            preferred_element_type=jnp.float32,
        )
        return (product * normalizer).reshape(pieces, piece_rows, panel)

    def partner_copy(dest):
        return pltpu.make_async_remote_copy(
            src_ref=to_partner.at[dest],
            dst_ref=from_partner.at[dest],
            send_sem=partner_send.at[dest],
            recv_sem=partner_recv.at[dest],
            device_id={"pair": partner},
            device_id_type=MESH,
        )

    def chain_copy(way, dest, piece):
        return pltpu.make_async_remote_copy(
            src_ref=sums.at[dest, piece],
            dst_ref=arrived.at[way, dest, piece],
            send_sem=chain_send.at[dest, piece],
            recv_sem=chain_recv.at[way, dest, piece],
            device_id={"pair": place + 2 - 4 * way},
            device_id_type=MESH,
        )

    def peer_copy(offset, piece):
        return pltpu.make_async_remote_copy(
            src_ref=sums.at[z, piece],
            dst_ref=peers_in.at[offset - 1, piece],
            send_sem=peer_send.at[offset - 1, piece],
            recv_sem=peer_recv.at[offset - 1, piece],
            device_id={"tm": (me + offset) % times},
            device_id_type=MESH,
        )

    low_half = (z < (chips + 1) // 2).astype(jnp.int32)

    def slab_step(step, carry):
        last = (step == chips - 1).astype(jnp.int32)
        falling = chips - 1 - step
        falling = falling - (falling <= z).astype(jnp.int32)
        rising = step + (step >= z).astype(jnp.int32)
        dest = last * z + (1 - last) * (low_half * falling + (1 - low_half) * rising)
        to_partner[dest] = panel_slab(dest * 2 + 1 - core)
        partner_copy(dest).start()
        sums[dest] = panel_slab(dest * 2 + core)
        partner_copy(dest).wait_recv()

        def piece_step(piece, inner):
            sums[dest, piece] = sums[dest, piece] + from_partner[dest, piece]

            @pl.when(jnp.logical_and(z == 0, dest > 0))
            def _():
                chain_copy(0, dest, piece).start()

            @pl.when(jnp.logical_and(z == chips - 1, dest < chips - 1))
            def _():
                chain_copy(1, dest, piece).start()

            return inner

        lax.fori_loop(0, pieces, piece_step, 0)
        return carry

    lax.fori_loop(0, chips, slab_step, 0)

    blocks, per_block, cb = coulomb_ref.shape[0], coulomb_ref.shape[1], coulomb_ref.shape[2]
    for block in range(blocks):
        factor = coulomb_ref[block].reshape(per_block * cb, cb)
        high = factor.astype(jnp.bfloat16)
        coulomb_high[block] = high
        coulomb_low[block] = (factor - high.astype(jnp.float32)).astype(jnp.bfloat16)

    from_below = (z > 0).astype(jnp.int32) * (chips - 1 - z)
    from_above = (z < chips - 1).astype(jnp.int32) * z
    finish = jnp.maximum(from_below, from_above)

    def chain_step(index, carry):
        step = index // pieces
        piece = index % pieces
        for way in (0, 1):
            dest = (chips - 1 - step) if way == 0 else step
            if way == 0:
                here = jnp.logical_and(z > 0, dest >= z)
            else:
                here = jnp.logical_and(z < chips - 1, dest <= z)

            @pl.when(here)
            def _():
                chain_copy(way, dest, piece).wait_recv()
                sums[dest, piece] = sums[dest, piece] + arrived[way, dest, piece]

                @pl.when(dest != z)
                def _():
                    chain_copy(way, dest, piece).start()

        @pl.when(step == finish)
        def _():
            for offset in range(1, times):
                peer_copy(offset, piece).start()

        return carry

    lax.fori_loop(0, chips * pieces, chain_step, 0)

    def mix_step(piece, carry):
        mixed = sums[z, piece] * weights_ref[me, me]
        for offset in range(1, times):
            peer_copy(offset, piece).wait_recv()
            mixed = mixed + peers_in[offset - 1, piece] * weights_ref[me, (me + times - offset) % times]
        at = pl.ds(pl.multiple_of(piece * piece_rows, piece_rows), piece_rows)
        for block in range(blocks):
            spectra[block, at, :] = mixed[:, block * cb : (block + 1) * cb]
        return carry

    lax.fori_loop(0, pieces, mix_step, 0)

    for block in range(blocks):
        gathered = jnp.concatenate(
            [spectra[factor_rows_ref[block, k]] for k in range(per_block)], axis=1
        )
        high = gathered.astype(jnp.bfloat16)
        low = (gathered - high.astype(jnp.float32)).astype(jnp.bfloat16)
        total = jnp.dot(high, coulomb_high[block], preferred_element_type=jnp.float32)
        total += jnp.dot(low, coulomb_high[block], preferred_element_type=jnp.float32)
        total += jnp.dot(high, coulomb_low[block], preferred_element_type=jnp.float32)
        out_ref[0, :, block * cb : (block + 1) * cb] = total

    def close_step(dest, carry):
        partner_copy(dest).wait_send()

        @pl.when(dest != z)
        def _():
            def close_piece(piece, inner):
                chain_copy(0, dest, piece).wait_send()
                return inner

            lax.fori_loop(0, pieces, close_piece, 0)

        return carry

    lax.fori_loop(0, chips, close_step, 0)

    def close_peers(piece, carry):
        for offset in range(1, times):
            peer_copy(offset, piece).wait_send()
        return carry

    lax.fori_loop(0, pieces, close_peers, 0)


def kernel_form(
    times,
    pair_devices,
    three_center,
    green_occ,
    green_vir,
    pair_list,
    block_counts,
    cosine_weights,
    coulomb_rows,
    coulomb_blocks,
):
    slots, width, panel = three_center.shape
    chips = pair_devices // 2
    rows = panel // pair_devices
    pieces = max(1, rows // 16)
    piece_rows = rows // pieces
    blocks, per_block, cb, _ = coulomb_blocks.shape
    normalizer = 1.0 / math.sqrt(slots * width * pair_devices)
    smem = pl.BlockSpec(memory_space=pltpu.SMEM)
    vmem = pl.BlockSpec(memory_space=pltpu.VMEM)
    slab = (pieces, piece_rows, panel)
    return pl.pallas_call(
        functools.partial(kernel, times, chips, normalizer),
        out_shape=jax.ShapeDtypeStruct((1, rows, panel), jnp.float32),
        in_specs=[smem] * 4 + [vmem] * 4,
        out_specs=vmem,
        scratch_shapes=[
            pltpu.VMEM((slots * width, panel), jnp.bfloat16),
            pltpu.VMEM((slots * width, panel), jnp.bfloat16),
            pltpu.VMEM((chips,) + slab, jnp.float32),
            pltpu.VMEM((chips,) + slab, jnp.float32),
            pltpu.VMEM((chips,) + slab, jnp.float32),
            pltpu.VMEM((2, chips) + slab, jnp.float32),
            pltpu.VMEM((times - 1,) + slab, jnp.float32),
            pltpu.VMEM((blocks, rows, cb), jnp.float32),
            pltpu.VMEM((blocks, per_block * cb, cb), jnp.bfloat16),
            pltpu.VMEM((blocks, per_block * cb, cb), jnp.bfloat16),
            pltpu.SemaphoreType.DMA((chips,)),
            pltpu.SemaphoreType.DMA((chips,)),
            pltpu.SemaphoreType.DMA((chips, pieces)),
            pltpu.SemaphoreType.DMA((2, chips, pieces)),
            pltpu.SemaphoreType.DMA((times - 1, pieces)),
            pltpu.SemaphoreType.DMA((times - 1, pieces)),
        ],
        compiler_params=pltpu.CompilerParams(
            collective_id=0, has_side_effects=True, vmem_limit_bytes=60 * 1024 * 1024
        ),
    )(
        pair_list,
        block_counts,
        cosine_weights,
        coulomb_rows,
        three_center,
        green_occ,
        green_vir,
        coulomb_blocks,
    )


def solution(mesh):
    times, pair_devices = mesh.shape["tm"], mesh.shape["pair"]

    def local(*args):
        rows = args[0].shape[2] // pair_devices
        short = 4 <= pair_devices <= 16 and 2 <= times <= 4
        if short and pair_devices % 2 == 0 and rows % 128 == 0:
            return kernel_form(times, pair_devices, *args)
        return collective_form(*args)

    return jax.shard_map(
        local,
        mesh=mesh,
        in_specs=(
            P("pair", None, None),
            P("tm", None, None, None),
            P("tm", None, None, None),
            P("pair"),
            P("pair"),
            P(),
            P(),
            P(),
        ),
        out_specs=P("tm", "pair", None),
        check_vma=False,
    )
```

```python
import functools
import math

import jax
import jax.numpy as jnp
from jax import lax
from jax.experimental import pallas as pl
from jax.experimental.pallas import tpu as pltpu
from jax.sharding import PartitionSpec as P

MESH = pl.DeviceIdType.MESH
SPREAD = 3
LAG = 2


def slab_order(chips):
    order, slots = [], []
    for z in range(chips):
        need = []
        for dest in range(chips):
            at = []
            if dest > z or (dest == z and z > 0):
                at.append(SPREAD * (chips - 1 - dest) + LAG * max(z - 1, 0))
            if dest < z or (dest == z and z < chips - 1):
                at.append(SPREAD * dest + LAG * max(chips - 2 - z, 0))
            need.append((min(at), dest))
        need.sort()
        order.append([dest for _, dest in need])
        slots.append([at for at, _ in need])
    return order, [min(column) for column in zip(*slots)]


def half_product(green_matrix, pair_list, alive_mask, three_center):
    picked = green_matrix[0][pair_list]
    product = jnp.einsum("bij,bjp->bip", picked, three_center, preferred_element_type=jnp.float32)
    product = product * alive_mask[:, None, None]
    return product.astype(jnp.bfloat16).reshape(-1, three_center.shape[2])


def collective_form(
    three_center,
    green_occ,
    green_vir,
    pair_list,
    block_counts,
    cosine_weights,
    coulomb_rows,
    coulomb_blocks,
):
    slots = three_center.shape[0]
    pair_devices = lax.axis_size("pair")
    alive_mask = (jnp.arange(slots, dtype=jnp.int32) < block_counts[0]).astype(jnp.float32)
    left_side = half_product(green_occ, pair_list, alive_mask, three_center)
    right_side = half_product(green_vir, pair_list, alive_mask, three_center)
    normalizer = 1.0 / math.sqrt(slots * three_center.shape[1] * pair_devices)
    summed = lax.dot_general(
        left_side, right_side, (((0,), (0,)), ((), ())), preferred_element_type=jnp.float32
    )
    row_slab = lax.psum_scatter(summed * normalizer, "pair", scatter_dimension=0, tiled=True)
    transformed = jnp.einsum(
        "ft,trc->frc",
        cosine_weights,
        lax.all_to_all(row_slab[None], "tm", split_axis=2, concat_axis=0, tiled=True),
        precision=lax.Precision.HIGHEST,
    )
    spectra = lax.all_to_all(transformed, "tm", split_axis=0, concat_axis=2, tiled=True)
    rows_here = spectra.shape[1]
    column_blocks = coulomb_rows.shape[0]
    per_column = coulomb_rows.shape[1]
    block_width = coulomb_blocks.shape[2]
    blocked = spectra.reshape(rows_here, column_blocks, block_width)
    gathered = jnp.take(blocked, coulomb_rows.reshape(-1), axis=1)
    factors = coulomb_blocks.reshape(column_blocks * per_column, block_width, block_width)
    screened = jnp.einsum("mjx,jxy->mjy", gathered, factors, precision=lax.Precision.HIGHEST)
    screened = screened.reshape(rows_here, column_blocks, per_column, block_width).sum(axis=2)
    return screened.reshape(1, rows_here, column_blocks * block_width)


def kernel(
    times,
    chips,
    normalizer,
    pair_list_ref,
    counts_ref,
    weights_ref,
    factor_rows_ref,
    three_ref,
    occ_ref,
    vir_ref,
    coulomb_ref,
    out_ref,
    left,
    right,
    to_partner,
    from_partner,
    sums,
    arrived,
    peers_in,
    spectra,
    coulomb_high,
    coulomb_low,
    partner_send,
    partner_recv,
    chain_send,
    chain_recv,
    peer_send,
    peer_recv,
):
    slots, width, panel = three_ref.shape
    pieces, piece_rows = sums.shape[1], sums.shape[2]
    rows = pieces * piece_rows
    me = lax.axis_index("tm")
    place = lax.axis_index("pair")
    z = place // 2
    core = place % 2
    partner = z * 2 + 1 - core

    barrier = pltpu.get_barrier_semaphore()
    pl.semaphore_signal(barrier, inc=1, device_id={"pair": partner}, device_id_type=MESH)
    for offset in range(1, times):
        pl.semaphore_signal(
            barrier, inc=1, device_id={"tm": (me + offset) % times}, device_id_type=MESH
        )

    @pl.when(z > 0)
    def _():
        pl.semaphore_signal(barrier, inc=1, device_id={"pair": place - 2}, device_id_type=MESH)

    @pl.when(z < chips - 1)
    def _():
        pl.semaphore_signal(barrier, inc=1, device_id={"pair": place + 2}, device_id_type=MESH)

    def half(slot, carry):
        group = pair_list_ref[slot]
        alive = (slot < counts_ref[0]).astype(jnp.float32)
        both = jnp.concatenate([occ_ref[0, group], vir_ref[0, group]], axis=0)
        product = jnp.dot(both, three_ref[slot], preferred_element_type=jnp.float32) * alive
        product = product.astype(jnp.bfloat16)
        here = pl.ds(pl.multiple_of(slot * width, width), width)
        left[here, :] = product[:width]
        right[here, :] = product[width:]
        return carry

    lax.fori_loop(0, slots, half, 0)

    neighbours = (z > 0).astype(jnp.int32) + (z < chips - 1).astype(jnp.int32)
    pl.semaphore_wait(barrier, times + neighbours)

    def panel_slab(slab):
        columns = pl.ds(pl.multiple_of(slab * rows, rows), rows)
        product = lax.dot_general(
            left[:, columns],
            right[...],
            (((0,), (0,)), ((), ())),
            preferred_element_type=jnp.float32,
        )
        return (product * normalizer).reshape(pieces, piece_rows, panel)

    def partner_copy(dest):
        return pltpu.make_async_remote_copy(
            src_ref=to_partner.at[dest],
            dst_ref=from_partner.at[dest],
            send_sem=partner_send.at[dest],
            recv_sem=partner_recv.at[dest],
            device_id={"pair": partner},
            device_id_type=MESH,
        )

    def chain_copy(way, dest, piece):
        return pltpu.make_async_remote_copy(
            src_ref=sums.at[dest, piece],
            dst_ref=arrived.at[way, dest, piece],
            send_sem=chain_send.at[dest, piece],
            recv_sem=chain_recv.at[way, dest, piece],
            device_id={"pair": place + 2 - 4 * way},
            device_id_type=MESH,
        )

    def peer_copy(offset, piece):
        return pltpu.make_async_remote_copy(
            src_ref=sums.at[z, piece],
            dst_ref=peers_in.at[offset - 1, piece],
            send_sem=peer_send.at[offset - 1, piece],
            recv_sem=peer_recv.at[offset - 1, piece],
            device_id={"tm": (me + offset) % times},
            device_id_type=MESH,
        )

    blocks, per_block, cb = coulomb_ref.shape[0], coulomb_ref.shape[1], coulomb_ref.shape[2]

    def split_factor():
        for block in range(blocks):
            factor = coulomb_ref[block].reshape(per_block * cb, cb)
            high = factor.astype(jnp.bfloat16)
            coulomb_high[block] = high
            coulomb_low[block] = (factor - high.astype(jnp.float32)).astype(jnp.bfloat16)

    order, ready = slab_order(chips)

    def slab_step(step, carry):
        dest = 0
        for row in range(chips):
            for k in range(chips):
                hit = jnp.logical_and(z == row, step == k).astype(jnp.int32)
                dest = dest + order[row][k] * hit
        to_partner[dest] = panel_slab(dest * 2 + 1 - core)
        partner_copy(dest).start()
        sums[dest] = panel_slab(dest * 2 + core)
        partner_copy(dest).wait_recv()
        sums[dest] = sums[dest] + from_partner[dest]
        return carry

    lag_up = LAG * jnp.maximum(z - 1, 0)
    lag_down = LAG * jnp.maximum(chips - 2 - z, 0)
    from_below = (z > 0).astype(jnp.int32) * (SPREAD * (chips - 1 - z) + lag_up)
    from_above = (z < chips - 1).astype(jnp.int32) * (SPREAD * z + lag_down)
    finish = jnp.maximum(from_below, from_above)

    def slot_step(slot, carry):
        first = sum((slot > at).astype(jnp.int32) for at in ready)
        after = sum((slot >= at).astype(jnp.int32) for at in ready)
        lax.fori_loop(first, after, slab_step, 0)

        def rank_step(rank, inner):
            for way in (0, 1):
                if way == 0:
                    dest = chips - 1 - rank
                    piece = slot - SPREAD * rank - lag_up
                    waits = jnp.logical_and(z > 0, dest >= z)
                    sends = dest > z
                else:
                    dest = rank
                    piece = slot - SPREAD * rank - lag_down
                    waits = jnp.logical_and(z < chips - 1, dest <= z)
                    sends = dest < z
                live = jnp.logical_and(piece >= 0, piece < pieces)

                @pl.when(jnp.logical_and(live, waits))
                def _():
                    chain_copy(way, dest, piece).wait_recv()
                    sums[dest, piece] = sums[dest, piece] + arrived[way, dest, piece]

                @pl.when(jnp.logical_and(live, sends))
                def _():
                    chain_copy(way, dest, piece).start()

            return inner

        lax.fori_loop(0, chips, rank_step, 0)

        done = slot - finish

        @pl.when(jnp.logical_and(done >= 0, done < pieces))
        def _():
            for offset in range(1, times):
                peer_copy(offset, done).start()

        @pl.when(slot == ready[-1] + 1)
        def _():
            split_factor()

        return carry

    lax.fori_loop(0, pieces + (SPREAD + LAG) * (chips - 1), slot_step, 0)

    def mix_step(piece, carry):
        mixed = sums[z, piece] * weights_ref[me, me]
        for offset in range(1, times):
            peer_copy(offset, piece).wait_recv()
            mixed = mixed + peers_in[offset - 1, piece] * weights_ref[me, (me + times - offset) % times]
        at = pl.ds(pl.multiple_of(piece * piece_rows, piece_rows), piece_rows)
        for block in range(blocks):
            spectra[block, at, :] = mixed[:, block * cb : (block + 1) * cb]
        return carry

    lax.fori_loop(0, pieces, mix_step, 0)

    for block in range(blocks):
        gathered = jnp.concatenate(
            [spectra[factor_rows_ref[block, k]] for k in range(per_block)], axis=1
        )
        high = gathered.astype(jnp.bfloat16)
        low = (gathered - high.astype(jnp.float32)).astype(jnp.bfloat16)
        total = jnp.dot(high, coulomb_high[block], preferred_element_type=jnp.float32)
        total += jnp.dot(low, coulomb_high[block], preferred_element_type=jnp.float32)
        total += jnp.dot(high, coulomb_low[block], preferred_element_type=jnp.float32)
        out_ref[0, :, block * cb : (block + 1) * cb] = total

    def close_step(dest, carry):
        partner_copy(dest).wait_send()

        @pl.when(dest != z)
        def _():
            def close_piece(piece, inner):
                chain_copy(0, dest, piece).wait_send()
                return inner

            lax.fori_loop(0, pieces, close_piece, 0)

        return carry

    lax.fori_loop(0, chips, close_step, 0)

    def close_peers(piece, carry):
        for offset in range(1, times):
            peer_copy(offset, piece).wait_send()
        return carry

    lax.fori_loop(0, pieces, close_peers, 0)


def kernel_form(
    times,
    pair_devices,
    three_center,
    green_occ,
    green_vir,
    pair_list,
    block_counts,
    cosine_weights,
    coulomb_rows,
    coulomb_blocks,
):
    slots, width, panel = three_center.shape
    chips = pair_devices // 2
    rows = panel // pair_devices
    pieces = max(1, rows // 16)
    piece_rows = rows // pieces
    blocks, per_block, cb, _ = coulomb_blocks.shape
    normalizer = 1.0 / math.sqrt(slots * width * pair_devices)
    smem = pl.BlockSpec(memory_space=pltpu.SMEM)
    vmem = pl.BlockSpec(memory_space=pltpu.VMEM)
    slab = (pieces, piece_rows, panel)
    return pl.pallas_call(
        functools.partial(kernel, times, chips, normalizer),
        out_shape=jax.ShapeDtypeStruct((1, rows, panel), jnp.float32),
        in_specs=[smem] * 4 + [vmem] * 4,
        out_specs=vmem,
        scratch_shapes=[
            pltpu.VMEM((slots * width, panel), jnp.bfloat16),
            pltpu.VMEM((slots * width, panel), jnp.bfloat16),
            pltpu.VMEM((chips,) + slab, jnp.float32),
            pltpu.VMEM((chips,) + slab, jnp.float32),
            pltpu.VMEM((chips,) + slab, jnp.float32),
            pltpu.VMEM((2, chips) + slab, jnp.float32),
            pltpu.VMEM((times - 1,) + slab, jnp.float32),
            pltpu.VMEM((blocks, rows, cb), jnp.float32),
            pltpu.VMEM((blocks, per_block * cb, cb), jnp.bfloat16),
            pltpu.VMEM((blocks, per_block * cb, cb), jnp.bfloat16),
            pltpu.SemaphoreType.DMA((chips,)),
            pltpu.SemaphoreType.DMA((chips,)),
            pltpu.SemaphoreType.DMA((chips, pieces)),
            pltpu.SemaphoreType.DMA((2, chips, pieces)),
            pltpu.SemaphoreType.DMA((times - 1, pieces)),
            pltpu.SemaphoreType.DMA((times - 1, pieces)),
        ],
        compiler_params=pltpu.CompilerParams(
            collective_id=0, has_side_effects=True, vmem_limit_bytes=60 * 1024 * 1024
        ),
    )(
        pair_list,
        block_counts,
        cosine_weights,
        coulomb_rows,
        three_center,
        green_occ,
        green_vir,
        coulomb_blocks,
    )


def solution(mesh):
    times, pair_devices = mesh.shape["tm"], mesh.shape["pair"]

    def local(*args):
        rows = args[0].shape[2] // pair_devices
        short = 4 <= pair_devices <= 16 and 2 <= times <= 4
        if short and pair_devices % 2 == 0 and rows % 128 == 0:
            return kernel_form(times, pair_devices, *args)
        return collective_form(*args)

    return jax.shard_map(
        local,
        mesh=mesh,
        in_specs=(
            P("pair", None, None),
            P("tm", None, None, None),
            P("tm", None, None, None),
            P("pair"),
            P("pair"),
            P(),
            P(),
            P(),
        ),
        out_specs=P("tm", "pair", None),
        check_vma=False,
    )
```

```python
import functools
import math

import jax
import jax.numpy as jnp
from jax import lax
from jax.experimental import pallas as pl
from jax.experimental.pallas import tpu as pltpu
from jax.sharding import PartitionSpec as P

MESH = pl.DeviceIdType.MESH
SPREAD = 3
LAG = 3


def slab_order(chips):
    order, slots = [], []
    for z in range(chips):
        need = []
        for dest in range(chips):
            at = []
            if dest > z or (dest == z and z > 0):
                at.append(SPREAD * (chips - 1 - dest) + LAG * max(z - 1, 0))
            if dest < z or (dest == z and z < chips - 1):
                at.append(SPREAD * dest + LAG * max(chips - 2 - z, 0))
            need.append((min(at), dest))
        need.sort()
        order.append([dest for _, dest in need])
        slots.append([at for at, _ in need])
    return order, [min(column) for column in zip(*slots)]


def half_product(green_matrix, pair_list, alive_mask, three_center):
    picked = green_matrix[0][pair_list]
    product = jnp.einsum("bij,bjp->bip", picked, three_center, preferred_element_type=jnp.float32)
    product = product * alive_mask[:, None, None]
    return product.astype(jnp.bfloat16).reshape(-1, three_center.shape[2])


def collective_form(
    three_center,
    green_occ,
    green_vir,
    pair_list,
    block_counts,
    cosine_weights,
    coulomb_rows,
    coulomb_blocks,
):
    slots = three_center.shape[0]
    pair_devices = lax.axis_size("pair")
    alive_mask = (jnp.arange(slots, dtype=jnp.int32) < block_counts[0]).astype(jnp.float32)
    left_side = half_product(green_occ, pair_list, alive_mask, three_center)
    right_side = half_product(green_vir, pair_list, alive_mask, three_center)
    normalizer = 1.0 / math.sqrt(slots * three_center.shape[1] * pair_devices)
    summed = lax.dot_general(
        left_side, right_side, (((0,), (0,)), ((), ())), preferred_element_type=jnp.float32
    )
    row_slab = lax.psum_scatter(summed * normalizer, "pair", scatter_dimension=0, tiled=True)
    transformed = jnp.einsum(
        "ft,trc->frc",
        cosine_weights,
        lax.all_to_all(row_slab[None], "tm", split_axis=2, concat_axis=0, tiled=True),
        precision=lax.Precision.HIGHEST,
    )
    spectra = lax.all_to_all(transformed, "tm", split_axis=0, concat_axis=2, tiled=True)
    rows_here = spectra.shape[1]
    column_blocks = coulomb_rows.shape[0]
    per_column = coulomb_rows.shape[1]
    block_width = coulomb_blocks.shape[2]
    blocked = spectra.reshape(rows_here, column_blocks, block_width)
    gathered = jnp.take(blocked, coulomb_rows.reshape(-1), axis=1)
    factors = coulomb_blocks.reshape(column_blocks * per_column, block_width, block_width)
    screened = jnp.einsum("mjx,jxy->mjy", gathered, factors, precision=lax.Precision.HIGHEST)
    screened = screened.reshape(rows_here, column_blocks, per_column, block_width).sum(axis=2)
    return screened.reshape(1, rows_here, column_blocks * block_width)


def kernel(
    times,
    chips,
    normalizer,
    pair_list_ref,
    counts_ref,
    weights_ref,
    factor_rows_ref,
    three_ref,
    occ_ref,
    vir_ref,
    coulomb_ref,
    out_ref,
    left,
    right,
    to_partner,
    from_partner,
    sums,
    arrived,
    peers_in,
    spectra,
    coulomb_high,
    coulomb_low,
    partner_send,
    partner_recv,
    chain_send,
    chain_recv,
    peer_send,
    peer_recv,
):
    slots, width, panel = three_ref.shape
    pieces, piece_rows = sums.shape[1], sums.shape[2]
    rows = pieces * piece_rows
    me = lax.axis_index("tm")
    place = lax.axis_index("pair")
    z = place // 2
    core = place % 2
    partner = z * 2 + 1 - core

    barrier = pltpu.get_barrier_semaphore()
    pl.semaphore_signal(barrier, inc=1, device_id={"pair": partner}, device_id_type=MESH)
    for offset in range(1, times):
        pl.semaphore_signal(
            barrier, inc=1, device_id={"tm": (me + offset) % times}, device_id_type=MESH
        )

    @pl.when(z > 0)
    def _():
        pl.semaphore_signal(barrier, inc=1, device_id={"pair": place - 2}, device_id_type=MESH)

    @pl.when(z < chips - 1)
    def _():
        pl.semaphore_signal(barrier, inc=1, device_id={"pair": place + 2}, device_id_type=MESH)

    def half(slot, carry):
        group = pair_list_ref[slot]
        alive = (slot < counts_ref[0]).astype(jnp.float32)
        both = jnp.concatenate([occ_ref[0, group], vir_ref[0, group]], axis=0)
        product = jnp.dot(both, three_ref[slot], preferred_element_type=jnp.float32) * alive
        product = product.astype(jnp.bfloat16)
        here = pl.ds(pl.multiple_of(slot * width, width), width)
        left[here, :] = product[:width]
        right[here, :] = product[width:]
        return carry

    lax.fori_loop(0, slots, half, 0)

    neighbours = (z > 0).astype(jnp.int32) + (z < chips - 1).astype(jnp.int32)
    pl.semaphore_wait(barrier, times + neighbours)

    def panel_slab(slab):
        columns = pl.ds(pl.multiple_of(slab * rows, rows), rows)
        product = lax.dot_general(
            left[:, columns],
            right[...],
            (((0,), (0,)), ((), ())),
            preferred_element_type=jnp.float32,
        )
        return (product * normalizer).reshape(pieces, piece_rows, panel)

    def partner_copy(dest):
        return pltpu.make_async_remote_copy(
            src_ref=to_partner.at[dest],
            dst_ref=from_partner.at[dest],
            send_sem=partner_send.at[dest],
            recv_sem=partner_recv.at[dest],
            device_id={"pair": partner},
            device_id_type=MESH,
        )

    def chain_copy(way, dest, piece):
        return pltpu.make_async_remote_copy(
            src_ref=sums.at[dest, piece],
            dst_ref=arrived.at[way, dest, piece],
            send_sem=chain_send.at[dest, piece],
            recv_sem=chain_recv.at[way, dest, piece],
            device_id={"pair": place + 2 - 4 * way},
            device_id_type=MESH,
        )

    def peer_copy(offset, piece):
        return pltpu.make_async_remote_copy(
            src_ref=sums.at[z, piece],
            dst_ref=peers_in.at[offset - 1, piece],
            send_sem=peer_send.at[offset - 1, piece],
            recv_sem=peer_recv.at[offset - 1, piece],
            device_id={"tm": (me + offset) % times},
            device_id_type=MESH,
        )

    blocks, per_block, cb = coulomb_ref.shape[0], coulomb_ref.shape[1], coulomb_ref.shape[2]

    def split_factor():
        for block in range(blocks):
            factor = coulomb_ref[block].reshape(per_block * cb, cb)
            high = factor.astype(jnp.bfloat16)
            coulomb_high[block] = high
            coulomb_low[block] = (factor - high.astype(jnp.float32)).astype(jnp.bfloat16)

    order, ready = slab_order(chips)

    def slab_step(step, carry):
        dest = 0
        for row in range(chips):
            for k in range(chips):
                hit = jnp.logical_and(z == row, step == k).astype(jnp.int32)
                dest = dest + order[row][k] * hit
        to_partner[dest] = panel_slab(dest * 2 + 1 - core)
        partner_copy(dest).start()
        sums[dest] = panel_slab(dest * 2 + core)
        partner_copy(dest).wait_recv()
        sums[dest] = sums[dest] + from_partner[dest]
        return carry

    lag_up = LAG * jnp.maximum(z - 1, 0)
    lag_down = LAG * jnp.maximum(chips - 2 - z, 0)
    from_below = (z > 0).astype(jnp.int32) * (SPREAD * (chips - 1 - z) + lag_up)
    from_above = (z < chips - 1).astype(jnp.int32) * (SPREAD * z + lag_down)
    finish = jnp.maximum(from_below, from_above)

    def slot_step(slot, carry):
        first = sum((slot > at).astype(jnp.int32) for at in ready)
        after = sum((slot >= at).astype(jnp.int32) for at in ready)
        lax.fori_loop(first, after, slab_step, 0)

        def rank_step(rank, inner):
            for way in (0, 1):
                if way == 0:
                    dest = chips - 1 - rank
                    piece = slot - SPREAD * rank - lag_up
                    waits = jnp.logical_and(z > 0, dest >= z)
                    sends = dest > z
                else:
                    dest = rank
                    piece = slot - SPREAD * rank - lag_down
                    waits = jnp.logical_and(z < chips - 1, dest <= z)
                    sends = dest < z
                live = jnp.logical_and(piece >= 0, piece < pieces)

                @pl.when(jnp.logical_and(live, waits))
                def _():
                    chain_copy(way, dest, piece).wait_recv()
                    sums[dest, piece] = sums[dest, piece] + arrived[way, dest, piece]

                @pl.when(jnp.logical_and(live, sends))
                def _():
                    chain_copy(way, dest, piece).start()

            return inner

        lax.fori_loop(0, chips, rank_step, 0)

        done = slot - finish

        @pl.when(jnp.logical_and(done >= 0, done < pieces))
        def _():
            for offset in range(1, times):
                peer_copy(offset, done).start()

        @pl.when(slot == ready[-1] + 1)
        def _():
            split_factor()

        return carry

    lax.fori_loop(0, pieces + (SPREAD + LAG) * (chips - 1), slot_step, 0)

    def mix_step(piece, carry):
        mixed = sums[z, piece] * weights_ref[me, me]
        for offset in range(1, times):
            peer_copy(offset, piece).wait_recv()
            mixed = mixed + peers_in[offset - 1, piece] * weights_ref[me, (me + times - offset) % times]
        at = pl.ds(pl.multiple_of(piece * piece_rows, piece_rows), piece_rows)
        for block in range(blocks):
            spectra[block, at, :] = mixed[:, block * cb : (block + 1) * cb]
        return carry

    lax.fori_loop(0, pieces, mix_step, 0)

    for block in range(blocks):
        gathered = jnp.concatenate(
            [spectra[factor_rows_ref[block, k]] for k in range(per_block)], axis=1
        )
        high = gathered.astype(jnp.bfloat16)
        low = (gathered - high.astype(jnp.float32)).astype(jnp.bfloat16)
        total = jnp.dot(high, coulomb_high[block], preferred_element_type=jnp.float32)
        total += jnp.dot(low, coulomb_high[block], preferred_element_type=jnp.float32)
        total += jnp.dot(high, coulomb_low[block], preferred_element_type=jnp.float32)
        out_ref[0, :, block * cb : (block + 1) * cb] = total

    def close_step(dest, carry):
        partner_copy(dest).wait_send()

        @pl.when(dest != z)
        def _():
            def close_piece(piece, inner):
                chain_copy(0, dest, piece).wait_send()
                return inner

            lax.fori_loop(0, pieces, close_piece, 0)

        return carry

    lax.fori_loop(0, chips, close_step, 0)

    def close_peers(piece, carry):
        for offset in range(1, times):
            peer_copy(offset, piece).wait_send()
        return carry

    lax.fori_loop(0, pieces, close_peers, 0)


def kernel_form(
    times,
    pair_devices,
    three_center,
    green_occ,
    green_vir,
    pair_list,
    block_counts,
    cosine_weights,
    coulomb_rows,
    coulomb_blocks,
):
    slots, width, panel = three_center.shape
    chips = pair_devices // 2
    rows = panel // pair_devices
    pieces = max(1, rows // 16)
    piece_rows = rows // pieces
    blocks, per_block, cb, _ = coulomb_blocks.shape
    normalizer = 1.0 / math.sqrt(slots * width * pair_devices)
    smem = pl.BlockSpec(memory_space=pltpu.SMEM)
    vmem = pl.BlockSpec(memory_space=pltpu.VMEM)
    slab = (pieces, piece_rows, panel)
    return pl.pallas_call(
        functools.partial(kernel, times, chips, normalizer),
        out_shape=jax.ShapeDtypeStruct((1, rows, panel), jnp.float32),
        in_specs=[smem] * 4 + [vmem] * 4,
        out_specs=vmem,
        scratch_shapes=[
            pltpu.VMEM((slots * width, panel), jnp.bfloat16),
            pltpu.VMEM((slots * width, panel), jnp.bfloat16),
            pltpu.VMEM((chips,) + slab, jnp.float32),
            pltpu.VMEM((chips,) + slab, jnp.float32),
            pltpu.VMEM((chips,) + slab, jnp.float32),
            pltpu.VMEM((2, chips) + slab, jnp.float32),
            pltpu.VMEM((times - 1,) + slab, jnp.float32),
            pltpu.VMEM((blocks, rows, cb), jnp.float32),
            pltpu.VMEM((blocks, per_block * cb, cb), jnp.bfloat16),
            pltpu.VMEM((blocks, per_block * cb, cb), jnp.bfloat16),
            pltpu.SemaphoreType.DMA((chips,)),
            pltpu.SemaphoreType.DMA((chips,)),
            pltpu.SemaphoreType.DMA((chips, pieces)),
            pltpu.SemaphoreType.DMA((2, chips, pieces)),
            pltpu.SemaphoreType.DMA((times - 1, pieces)),
            pltpu.SemaphoreType.DMA((times - 1, pieces)),
        ],
        compiler_params=pltpu.CompilerParams(
            collective_id=0, has_side_effects=True, vmem_limit_bytes=60 * 1024 * 1024
        ),
    )(
        pair_list,
        block_counts,
        cosine_weights,
        coulomb_rows,
        three_center,
        green_occ,
        green_vir,
        coulomb_blocks,
    )


def solution(mesh):
    times, pair_devices = mesh.shape["tm"], mesh.shape["pair"]

    def local(*args):
        rows = args[0].shape[2] // pair_devices
        short = 4 <= pair_devices <= 16 and 2 <= times <= 4
        if short and pair_devices % 2 == 0 and rows % 128 == 0:
            return kernel_form(times, pair_devices, *args)
        return collective_form(*args)

    return jax.shard_map(
        local,
        mesh=mesh,
        in_specs=(
            P("pair", None, None),
            P("tm", None, None, None),
            P("tm", None, None, None),
            P("pair"),
            P("pair"),
            P(),
            P(),
            P(),
        ),
        out_specs=P("tm", "pair", None),
        check_vma=False,
    )
```

```python
import functools
import math

import jax
import jax.numpy as jnp
from jax import lax
from jax.experimental import pallas as pl
from jax.experimental.pallas import tpu as pltpu
from jax.sharding import PartitionSpec as P

MESH = pl.DeviceIdType.MESH
SPREAD = 3
LAG = 3


def slab_order(chips):
    order, slots = [], []
    for z in range(chips):
        need = []
        for dest in range(chips):
            at = []
            if dest > z or (dest == z and z > 0):
                at.append(SPREAD * (chips - 1 - dest) + LAG * max(z - 1, 0))
            if dest < z or (dest == z and z < chips - 1):
                at.append(SPREAD * dest + LAG * max(chips - 2 - z, 0))
            need.append((min(at), dest))
        need.sort()
        order.append([dest for _, dest in need])
        slots.append([at for at, _ in need])
    return order, [min(column) for column in zip(*slots)]


def half_product(green_matrix, pair_list, alive_mask, three_center):
    picked = green_matrix[0][pair_list]
    product = jnp.einsum("bij,bjp->bip", picked, three_center, preferred_element_type=jnp.float32)
    product = product * alive_mask[:, None, None]
    return product.astype(jnp.bfloat16).reshape(-1, three_center.shape[2])


def collective_form(
    three_center,
    green_occ,
    green_vir,
    pair_list,
    block_counts,
    cosine_weights,
    coulomb_rows,
    coulomb_blocks,
):
    slots = three_center.shape[0]
    pair_devices = lax.axis_size("pair")
    alive_mask = (jnp.arange(slots, dtype=jnp.int32) < block_counts[0]).astype(jnp.float32)
    left_side = half_product(green_occ, pair_list, alive_mask, three_center)
    right_side = half_product(green_vir, pair_list, alive_mask, three_center)
    normalizer = 1.0 / math.sqrt(slots * three_center.shape[1] * pair_devices)
    summed = lax.dot_general(
        left_side, right_side, (((0,), (0,)), ((), ())), preferred_element_type=jnp.float32
    )
    row_slab = lax.psum_scatter(summed * normalizer, "pair", scatter_dimension=0, tiled=True)
    transformed = jnp.einsum(
        "ft,trc->frc",
        cosine_weights,
        lax.all_to_all(row_slab[None], "tm", split_axis=2, concat_axis=0, tiled=True),
        precision=lax.Precision.HIGHEST,
    )
    spectra = lax.all_to_all(transformed, "tm", split_axis=0, concat_axis=2, tiled=True)
    rows_here = spectra.shape[1]
    column_blocks = coulomb_rows.shape[0]
    per_column = coulomb_rows.shape[1]
    block_width = coulomb_blocks.shape[2]
    blocked = spectra.reshape(rows_here, column_blocks, block_width)
    gathered = jnp.take(blocked, coulomb_rows.reshape(-1), axis=1)
    factors = coulomb_blocks.reshape(column_blocks * per_column, block_width, block_width)
    screened = jnp.einsum("mjx,jxy->mjy", gathered, factors, precision=lax.Precision.HIGHEST)
    screened = screened.reshape(rows_here, column_blocks, per_column, block_width).sum(axis=2)
    return screened.reshape(1, rows_here, column_blocks * block_width)


def kernel(
    times,
    chips,
    normalizer,
    pair_list_ref,
    counts_ref,
    weights_ref,
    factor_rows_ref,
    three_ref,
    occ_ref,
    vir_ref,
    coulomb_hbm,
    out_ref,
    left,
    right,
    to_partner,
    from_partner,
    sums,
    arrived,
    peers_in,
    spectra,
    coulomb_high,
    coulomb_low,
    partner_send,
    partner_recv,
    chain_send,
    chain_recv,
    peer_send,
    peer_recv,
    factor,
    factor_sem,
):
    slots, width, panel = three_ref.shape
    pieces, piece_rows = sums.shape[1], sums.shape[2]
    rows = pieces * piece_rows
    me = lax.axis_index("tm")
    place = lax.axis_index("pair")
    z = place // 2
    core = place % 2
    partner = z * 2 + 1 - core

    factor_copy = pltpu.make_async_copy(coulomb_hbm, factor, factor_sem)
    factor_copy.start()

    barrier = pltpu.get_barrier_semaphore()
    pl.semaphore_signal(barrier, inc=1, device_id={"pair": partner}, device_id_type=MESH)
    for offset in range(1, times):
        pl.semaphore_signal(
            barrier, inc=1, device_id={"tm": (me + offset) % times}, device_id_type=MESH
        )

    @pl.when(z > 0)
    def _():
        pl.semaphore_signal(barrier, inc=1, device_id={"pair": place - 2}, device_id_type=MESH)

    @pl.when(z < chips - 1)
    def _():
        pl.semaphore_signal(barrier, inc=1, device_id={"pair": place + 2}, device_id_type=MESH)

    def half(slot, carry):
        group = pair_list_ref[slot]
        alive = (slot < counts_ref[0]).astype(jnp.float32)
        both = jnp.concatenate([occ_ref[0, group], vir_ref[0, group]], axis=0)
        product = jnp.dot(both, three_ref[slot], preferred_element_type=jnp.float32) * alive
        product = product.astype(jnp.bfloat16)
        here = pl.ds(pl.multiple_of(slot * width, width), width)
        left[here, :] = product[:width]
        right[here, :] = product[width:]
        return carry

    lax.fori_loop(0, slots, half, 0)

    neighbours = (z > 0).astype(jnp.int32) + (z < chips - 1).astype(jnp.int32)
    pl.semaphore_wait(barrier, times + neighbours)

    def panel_slab(slab):
        columns = pl.ds(pl.multiple_of(slab * rows, rows), rows)
        product = lax.dot_general(
            left[:, columns],
            right[...],
            (((0,), (0,)), ((), ())),
            preferred_element_type=jnp.float32,
        )
        return (product * normalizer).reshape(pieces, piece_rows, panel)

    def partner_copy(dest):
        return pltpu.make_async_remote_copy(
            src_ref=to_partner.at[dest],
            dst_ref=from_partner.at[dest],
            send_sem=partner_send.at[dest],
            recv_sem=partner_recv.at[dest],
            device_id={"pair": partner},
            device_id_type=MESH,
        )

    def chain_copy(way, dest, piece):
        return pltpu.make_async_remote_copy(
            src_ref=sums.at[dest, piece],
            dst_ref=arrived.at[way, dest, piece],
            send_sem=chain_send.at[dest, piece],
            recv_sem=chain_recv.at[way, dest, piece],
            device_id={"pair": place + 2 - 4 * way},
            device_id_type=MESH,
        )

    def peer_copy(offset, piece):
        return pltpu.make_async_remote_copy(
            src_ref=sums.at[z, piece],
            dst_ref=peers_in.at[offset - 1, piece],
            send_sem=peer_send.at[offset - 1, piece],
            recv_sem=peer_recv.at[offset - 1, piece],
            device_id={"tm": (me + offset) % times},
            device_id_type=MESH,
        )

    blocks, per_block, cb = factor.shape[0], factor.shape[1], factor.shape[2]

    def split_factor():
        for block in range(blocks):
            exact = factor[block].reshape(per_block * cb, cb)
            high = exact.astype(jnp.bfloat16)
            coulomb_high[block] = high
            coulomb_low[block] = (exact - high.astype(jnp.float32)).astype(jnp.bfloat16)

    order, ready = slab_order(chips)

    def slab_step(step, carry):
        dest = 0
        for row in range(chips):
            for k in range(chips):
                hit = jnp.logical_and(z == row, step == k).astype(jnp.int32)
                dest = dest + order[row][k] * hit
        to_partner[dest] = panel_slab(dest * 2 + 1 - core)
        partner_copy(dest).start()
        sums[dest] = panel_slab(dest * 2 + core)
        partner_copy(dest).wait_recv()
        sums[dest] = sums[dest] + from_partner[dest]
        return carry

    lag_up = LAG * jnp.maximum(z - 1, 0)
    lag_down = LAG * jnp.maximum(chips - 2 - z, 0)
    from_below = (z > 0).astype(jnp.int32) * (SPREAD * (chips - 1 - z) + lag_up)
    from_above = (z < chips - 1).astype(jnp.int32) * (SPREAD * z + lag_down)
    finish = jnp.maximum(from_below, from_above)

    def slot_step(slot, carry):
        first = sum((slot > at).astype(jnp.int32) for at in ready)
        after = sum((slot >= at).astype(jnp.int32) for at in ready)
        lax.fori_loop(first, after, slab_step, 0)

        def rank_step(rank, inner):
            for way in (0, 1):
                if way == 0:
                    dest = chips - 1 - rank
                    piece = slot - SPREAD * rank - lag_up
                    waits = jnp.logical_and(z > 0, dest >= z)
                    sends = dest > z
                else:
                    dest = rank
                    piece = slot - SPREAD * rank - lag_down
                    waits = jnp.logical_and(z < chips - 1, dest <= z)
                    sends = dest < z
                live = jnp.logical_and(piece >= 0, piece < pieces)

                @pl.when(jnp.logical_and(live, waits))
                def _():
                    chain_copy(way, dest, piece).wait_recv()
                    sums[dest, piece] = sums[dest, piece] + arrived[way, dest, piece]

                @pl.when(jnp.logical_and(live, sends))
                def _():
                    chain_copy(way, dest, piece).start()

            return inner

        lax.fori_loop(0, chips, rank_step, 0)

        done = slot - finish

        @pl.when(jnp.logical_and(done >= 0, done < pieces))
        def _():
            for offset in range(1, times):
                peer_copy(offset, done).start()

        @pl.when(slot == ready[-1] + 1)
        def _():
            factor_copy.wait()
            split_factor()

        return carry

    lax.fori_loop(0, pieces + (SPREAD + LAG) * (chips - 1), slot_step, 0)

    def mix_step(piece, carry):
        mixed = sums[z, piece] * weights_ref[me, me]
        for offset in range(1, times):
            peer_copy(offset, piece).wait_recv()
            mixed = mixed + peers_in[offset - 1, piece] * weights_ref[me, (me + times - offset) % times]
        at = pl.ds(pl.multiple_of(piece * piece_rows, piece_rows), piece_rows)
        for block in range(blocks):
            spectra[block, at, :] = mixed[:, block * cb : (block + 1) * cb]
        return carry

    lax.fori_loop(0, pieces, mix_step, 0)

    for block in range(blocks):
        gathered = jnp.concatenate(
            [spectra[factor_rows_ref[block, k]] for k in range(per_block)], axis=1
        )
        high = gathered.astype(jnp.bfloat16)
        low = (gathered - high.astype(jnp.float32)).astype(jnp.bfloat16)
        total = jnp.dot(high, coulomb_high[block], preferred_element_type=jnp.float32)
        total += jnp.dot(low, coulomb_high[block], preferred_element_type=jnp.float32)
        total += jnp.dot(high, coulomb_low[block], preferred_element_type=jnp.float32)
        out_ref[0, :, block * cb : (block + 1) * cb] = total

    def close_step(dest, carry):
        partner_copy(dest).wait_send()

        @pl.when(dest != z)
        def _():
            def close_piece(piece, inner):
                chain_copy(0, dest, piece).wait_send()
                return inner

            lax.fori_loop(0, pieces, close_piece, 0)

        return carry

    lax.fori_loop(0, chips, close_step, 0)

    def close_peers(piece, carry):
        for offset in range(1, times):
            peer_copy(offset, piece).wait_send()
        return carry

    lax.fori_loop(0, pieces, close_peers, 0)


def kernel_form(
    times,
    pair_devices,
    three_center,
    green_occ,
    green_vir,
    pair_list,
    block_counts,
    cosine_weights,
    coulomb_rows,
    coulomb_blocks,
):
    slots, width, panel = three_center.shape
    chips = pair_devices // 2
    rows = panel // pair_devices
    pieces = max(1, rows // 16)
    piece_rows = rows // pieces
    blocks, per_block, cb, _ = coulomb_blocks.shape
    normalizer = 1.0 / math.sqrt(slots * width * pair_devices)
    smem = pl.BlockSpec(memory_space=pltpu.SMEM)
    vmem = pl.BlockSpec(memory_space=pltpu.VMEM)
    slab = (pieces, piece_rows, panel)
    return pl.pallas_call(
        functools.partial(kernel, times, chips, normalizer),
        out_shape=jax.ShapeDtypeStruct((1, rows, panel), jnp.float32),
        in_specs=[smem] * 4 + [vmem] * 3 + [pl.BlockSpec(memory_space=pl.ANY)],
        out_specs=vmem,
        scratch_shapes=[
            pltpu.VMEM((slots * width, panel), jnp.bfloat16),
            pltpu.VMEM((slots * width, panel), jnp.bfloat16),
            pltpu.VMEM((chips,) + slab, jnp.float32),
            pltpu.VMEM((chips,) + slab, jnp.float32),
            pltpu.VMEM((chips,) + slab, jnp.float32),
            pltpu.VMEM((2, chips) + slab, jnp.float32),
            pltpu.VMEM((times - 1,) + slab, jnp.float32),
            pltpu.VMEM((blocks, rows, cb), jnp.float32),
            pltpu.VMEM((blocks, per_block * cb, cb), jnp.bfloat16),
            pltpu.VMEM((blocks, per_block * cb, cb), jnp.bfloat16),
            pltpu.SemaphoreType.DMA((chips,)),
            pltpu.SemaphoreType.DMA((chips,)),
            pltpu.SemaphoreType.DMA((chips, pieces)),
            pltpu.SemaphoreType.DMA((2, chips, pieces)),
            pltpu.SemaphoreType.DMA((times - 1, pieces)),
            pltpu.SemaphoreType.DMA((times - 1, pieces)),
            pltpu.VMEM(coulomb_blocks.shape, jnp.float32),
            pltpu.SemaphoreType.DMA,
        ],
        compiler_params=pltpu.CompilerParams(
            collective_id=0, has_side_effects=True, vmem_limit_bytes=60 * 1024 * 1024
        ),
    )(
        pair_list,
        block_counts,
        cosine_weights,
        coulomb_rows,
        three_center,
        green_occ,
        green_vir,
        coulomb_blocks,
    )


def solution(mesh):
    times, pair_devices = mesh.shape["tm"], mesh.shape["pair"]

    def local(*args):
        rows = args[0].shape[2] // pair_devices
        short = 4 <= pair_devices <= 16 and 2 <= times <= 4
        if short and pair_devices % 2 == 0 and rows % 128 == 0:
            return kernel_form(times, pair_devices, *args)
        return collective_form(*args)

    return jax.shard_map(
        local,
        mesh=mesh,
        in_specs=(
            P("pair", None, None),
            P("tm", None, None, None),
            P("tm", None, None, None),
            P("pair"),
            P("pair"),
            P(),
            P(),
            P(),
        ),
        out_specs=P("tm", "pair", None),
        check_vma=False,
    )
```
